32 devices in a mesh: tm: 4 (over z), query: 2 (over y), rec: 4 (over x, core).
Axes of the slice: x: 2, y: 2, z: 4, core: 2. Of those that a mesh axis runs over, the one named last changes fastest.
Arguments:
- frames: bfloat16 [4, 2048, 1024], P('rec', 'tm'), may hold values from -100 to 100
- queries: bfloat16 [4096, 1024], P('query'), may hold values from -10 to 10
- kernel: float32 [33, 4096], P(None, 'query'), may hold values from 0.01 to 0.12
- labels: int32 [4, 2048], P('rec', 'tm'), may hold values from 0 to 4095
- lengths: int32 [4], P('rec'), may hold values from 512 to 2048, as said below
Outputs:
- grad_frames: bfloat16 [4, 2048, 1024], P('rec', 'tm', 'query')
- grad_queries: bfloat16 [4096, 1024], P('query', 'rec')
- grad_kernel: float32 [33, 4096], P(None, 'query')
The draws below stay inside these ranges and needn't reach their ends.
Inputs may be any that keep to these rules, and one draw needn't show every extreme that they name: `lengths`: each entry counts the valid frames at the start of its recording; at least one recording has all 2048 frames valid.
All inputs are finite; a program needn't handle non-finite values.
Results may differ from the reference program's by a relative error of at most 0.0049.
Values sent between devices are 32-bit elements; how exact they have to be, the bound alone decides.
A program may use at most 64 MiB of HBM per device.

```python
import math
import jax
import jax.numpy as jnp
from jax import lax

W = 1024
NQ = 4096
TAPS = 33
HALF = 16
FRAMES = 2048
RECS = 4
N_QUERY = 2


def base_tables(key):
    table = jnp.clip(jax.random.normal(jax.random.fold_in(key, 11), (NQ, W), jnp.float32), -4.0, 4.0)
    blocks = jax.random.permutation(jax.random.fold_in(key, 12), N_QUERY)
    row_block = jnp.arange(NQ) // (NQ // N_QUERY)
    col_block = jnp.arange(W) // (W // N_QUERY)
    boost = jnp.where(col_block[None, :] == blocks[row_block][:, None], 2.5, 1.0)
    table = (table * boost).astype(jnp.bfloat16).astype(jnp.float32)
    kernel = jnp.exp(jax.random.uniform(jax.random.fold_in(key, 13), (TAPS, NQ), jnp.float32, math.log(0.01), math.log(0.12)))
    return (table, kernel)


def draw_queries(key, part):
    table, kernel = base_tables(key)
    return table.astype(jnp.bfloat16)


def draw_kernel(key, part):
    table, kernel = base_tables(key)
    return kernel


def draw_frames(key, part):
    noise = jnp.clip(jax.random.normal(jax.random.fold_in(key, 21), (RECS, FRAMES, W), jnp.float32), -6.0, 6.0)
    return noise.astype(jnp.bfloat16)


def draw_lengths(key, part):
    counts = jax.random.randint(jax.random.fold_in(key, 41), (RECS,), FRAMES // 4, FRAMES + 1)
    full_one = jax.random.randint(jax.random.fold_in(key, 42), (), 0, RECS)
    return jnp.where(jnp.arange(RECS) == full_one, FRAMES, counts).astype(jnp.int32)


def plant(entries, rng, smallest, largest):
    index_at = [jax.random.randint(jax.random.fold_in(rng, axis), (), 0, length) for axis, length in enumerate(entries.shape)]
    longest = entries.shape.index(max(entries.shape))
    next_to = index_at[:longest] + [(index_at[longest] + 1) % entries.shape[longest]] + index_at[longest + 1:]
    return entries.at[tuple(index_at)].set(smallest).at[tuple(next_to)].set(largest)


def setup_inputs(seed: int = 0) -> dict:
    key_list = jax.random.split(jax.random.key(seed), 6)
    frames = draw_frames(jax.random.fold_in(key_list[5], 71), 0)
    queries = draw_queries(jax.random.fold_in(key_list[5], 71), 0)
    kernel = draw_kernel(jax.random.fold_in(key_list[5], 71), 0)
    labels = plant(jax.random.randint(key_list[3], (RECS, FRAMES), 0, NQ), jax.random.fold_in(key_list[3], 1), 0, NQ - 1).astype(jnp.int32)
    lengths = draw_lengths(jax.random.fold_in(key_list[5], 71), 0)
    return {"frames": frames, "queries": queries, "kernel": kernel, "labels": labels, "lengths": lengths}


def reference(frames, queries, kernel, labels, lengths):
    logit_scale = 10.0 / math.sqrt(W)
    query_ids = jnp.arange(NQ, dtype=jnp.int32)
    frame_ids = jnp.arange(FRAMES, dtype=jnp.int32)

    def one_record(record_items):
        frame_rows, label_ids, length_now = record_items
        is_valid = frame_ids < length_now
        scores = jnp.dot(frame_rows, queries.T, preferred_element_type=jnp.float32) * logit_scale
        scores = jnp.where(is_valid[:, None], scores, 0.0)
        padded = jnp.pad(scores, ((HALF, HALF), (0, 0)))
        smooth = jnp.zeros((FRAMES, NQ), jnp.float32)
        for offset in range(TAPS):
            smooth = smooth + kernel[offset][None, :] * padded[offset:offset + FRAMES]
        softmax_out = jax.nn.softmax(smooth, axis=1)
        positive = (label_ids[:, None] == query_ids[None, :]).astype(jnp.float32)
        map_grad = jnp.where(is_valid[:, None], softmax_out - positive, 0.0)
        grad_pad = jnp.pad(map_grad, ((HALF, HALF), (0, 0)))
        score_grad = jnp.zeros((FRAMES, NQ), jnp.float32)
        for offset in range(TAPS):
            begin_row = 2 * HALF - offset
            score_grad = score_grad + kernel[offset][None, :] * grad_pad[begin_row:begin_row + FRAMES]
        score_grad = jnp.where(is_valid[:, None], score_grad, 0.0).astype(jnp.bfloat16)
        frame_grad = (jnp.dot(score_grad, queries, preferred_element_type=jnp.float32) * logit_scale).astype(jnp.bfloat16)
        query_part = lax.dot_general(score_grad, frame_rows, (((0,), (0,)), ((), ())), preferred_element_type=jnp.float32)
        kernel_part = jnp.stack([lax.optimization_barrier(jnp.sum(map_grad * padded[offset:offset + FRAMES], axis=0)) for offset in range(TAPS)])
        return (frame_grad, query_part, kernel_part)
    grad_frames, query_parts, kernel_parts = lax.map(one_record, (frames, labels, lengths))
    grad_queries = (lax.optimization_barrier(jnp.sum(query_parts, axis=0)) * logit_scale).astype(jnp.bfloat16)
    return (grad_frames, grad_queries, lax.optimization_barrier(jnp.sum(kernel_parts, axis=0)))
```

```python
import math

import jax
import jax.numpy as jnp
from jax import lax
from jax.sharding import PartitionSpec as P


def merged(x, axis, combine):
    peers = lax.axis_size(axis)
    step = 1
    while step < peers:
        swap = [(i, i ^ step) for i in range(peers)]
        x = combine(x, lax.ppermute(x, axis, swap))
        step *= 2
    return x


def halo_rows(x, axis, width):
    peers = lax.axis_size(axis)
    up = [(i, i + 1) for i in range(peers - 1)]
    down = [(i + 1, i) for i in range(peers - 1)]
    before = lax.ppermute(x[x.shape[0] - width :], axis, up)
    after = lax.ppermute(x[:width], axis, down)
    return lax.optimization_barrier((before, after))


def tap_sum(kernel, padded, row_count, flipped):
    tap_count = kernel.shape[0]
    running = jnp.zeros((row_count, padded.shape[1]), jnp.float32)
    for offset in range(tap_count):
        begin_row = tap_count - 1 - offset if flipped else offset
        running = running + kernel[offset][None, :] * padded[begin_row : begin_row + row_count]
    return running


def combine_stats(first_pair, second_pair):
    top_value = jnp.maximum(first_pair[0], second_pair[0])
    total_value = first_pair[1] * jnp.exp(first_pair[0] - top_value) + second_pair[1] * jnp.exp(
        second_pair[0] - top_value
    )
    return jnp.stack([top_value, total_value])


def row_softmax(smooth):
    local_top = jnp.max(smooth, axis=1)
    local_total = jnp.sum(jnp.exp(smooth - local_top[:, None]), axis=1)
    stats = merged(jnp.stack([local_top, local_total]), "query", combine_stats)
    top_value, total_value = stats[0], stats[1]
    return jnp.exp(smooth - top_value[:, None]) / total_value[:, None]


def per_device(frames, queries, kernel, labels, lengths):
    frame_rows = frames[0]
    label_ids = labels[0]
    length_now = lengths[0]
    row_count = frame_rows.shape[0]
    query_count = queries.shape[0]
    width = frame_rows.shape[1]
    tap_count = kernel.shape[0]
    rim_width = tap_count // 2
    logit_scale = 10.0 / math.sqrt(width)
    frame_start = lax.axis_index("tm") * row_count
    is_valid = frame_start + jnp.arange(row_count, dtype=jnp.int32) < length_now
    query_start = lax.axis_index("query") * query_count
    query_ids = query_start + jnp.arange(query_count, dtype=jnp.int32)
    halo = 2 * rim_width
    tagged = jnp.concatenate(
        [
            frame_rows.astype(jnp.float32),
            jnp.broadcast_to(label_ids.astype(jnp.float32)[:, None], (row_count, 128)),
        ],
        axis=1,
    )
    before, after = halo_rows(tagged, "tm", halo)
    rim_rows = jnp.concatenate([before[:, :width], after[:, :width]]).astype(jnp.bfloat16)

    def scored(rows):
        return (
            lax.dot_general(
                rows, queries, (((1,), (1,)), ((), ())), preferred_element_type=jnp.float32
            )
            * logit_scale
        )

    inner = scored(frame_rows)
    rim = scored(rim_rows)
    wide = jnp.concatenate([rim[:halo], inner, rim[halo:]])
    wide_frames = frame_start - halo + jnp.arange(row_count + 2 * halo, dtype=jnp.int32)
    wide_valid = (wide_frames >= 0) & (wide_frames < length_now)
    wide = jnp.where(wide_valid[:, None], wide, 0.0)
    label_pad = jnp.concatenate(
        [
            before[halo - rim_width :, width].astype(jnp.int32),
            label_ids,
            after[:rim_width, width].astype(jnp.int32),
        ]
    )
    ext_rows = row_count + 2 * rim_width
    ext_frames = frame_start - rim_width + jnp.arange(ext_rows, dtype=jnp.int32)
    ext_valid = (ext_frames >= 0) & (ext_frames < length_now)
    smooth = tap_sum(kernel, wide, ext_rows, False)
    softmax_out = row_softmax(smooth)
    positive = (label_pad[:, None] == query_ids[None, :]).astype(jnp.float32)
    grad_pad = jnp.where(ext_valid[:, None], softmax_out - positive, 0.0)
    map_grad = grad_pad[rim_width : rim_width + row_count]
    padded = wide[rim_width : rim_width + row_count + 2 * rim_width]
    score_grad = tap_sum(kernel, grad_pad, row_count, True)
    score_grad = jnp.where(is_valid[:, None], score_grad, 0.0).astype(jnp.bfloat16)
    frame_part = jnp.dot(score_grad, queries, preferred_element_type=jnp.float32)
    frame_sum = lax.psum_scatter(frame_part, "query", scatter_dimension=1, tiled=True)
    grad_frames = (frame_sum * logit_scale).astype(jnp.bfloat16)[None]
    query_part = lax.dot_general(
        score_grad, frame_rows, (((0,), (0,)), ((), ())), preferred_element_type=jnp.float32
    )
    kernel_part = jnp.stack(
        [
            jnp.sum(map_grad * padded[offset : offset + row_count], axis=0)
            for offset in range(tap_count)
        ]
    )
    query_cols = lax.psum_scatter(query_part, "rec", scatter_dimension=1, tiled=True)
    query_cols, grad_kernel = lax.psum((query_cols, lax.psum(kernel_part, "rec")), "tm")
    grad_queries = (query_cols * logit_scale).astype(jnp.bfloat16)
    return (grad_frames, grad_queries, grad_kernel)


def solution(mesh):
    in_specs = (P("rec", "tm", None), P("query", None), P(None, "query"), P("rec", "tm"), P("rec"))
    out_specs = (P("rec", "tm", "query"), P("query", "rec"), P(None, "query"))
    return jax.shard_map(
        per_device, mesh=mesh, in_specs=in_specs, out_specs=out_specs, check_vma=False
    )
```

```python
import functools
import math

import jax
import jax.numpy as jnp
from jax import lax
from jax.experimental import pallas as pl
from jax.experimental.pallas import tpu as pltpu
from jax.sharding import PartitionSpec as P


def merged(x, axis, combine):
    peers = lax.axis_size(axis)
    step = 1
    while step < peers:
        swap = [(i, i ^ step) for i in range(peers)]
        x = combine(x, lax.ppermute(x, axis, swap))
        step *= 2
    return x


def halo_rows(x, axis, width):
    peers = lax.axis_size(axis)
    up = [(i, i + 1) for i in range(peers - 1)]
    down = [(i + 1, i) for i in range(peers - 1)]
    before = lax.ppermute(x[x.shape[0] - width :], axis, up)
    after = lax.ppermute(x[:width], axis, down)
    return lax.optimization_barrier((before, after))


MESH = pl.DeviceIdType.MESH


def bit_reversed(p, bits):
    return sum(((p >> k) & 1) << (bits - 1 - k) for k in range(bits))


def gradient_kernel(
    dims, scale, sg_ref, fr_ref, qu_ref, kp_ref, gf_ref, gq_ref, gk_ref, *scratch
):
    tms, peers, recs, chunk = dims
    bits = recs.bit_length() - 1
    acc, scratch = scratch[:bits], scratch[bits:]
    arrived, scratch = scratch[:bits], scratch[bits:]
    kacc, scratch = scratch[:bits], scratch[bits:]
    karrived, scratch = scratch[:bits], scratch[bits:]
    (mid, outer, inner, kmid, kouter, kinner, fpart, fin) = scratch[:8]
    (rec_send, rec_recv, in_send, out_recv, out_send, inn_recv, f_send, f_recv) = scratch[8:]

    t = lax.axis_index("tm")
    y = lax.axis_index("query")
    r = lax.axis_index("rec")
    half = tms // 2
    low = t < half
    is_end = (t == 0) | (t == tms - 1)
    is_mid = (t == half - 1) | (t == half)
    inward = jnp.where(low, t + 1, t - 1)
    outward = jnp.where(low, lax.rem(t + tms - 1, tms), lax.rem(t + 1, tms))
    my_bits = [lax.rem(r // (1 << k), 2) for k in range(bits)]
    rec_peers = [r + (1 - 2 * my_bits[k]) * (1 << k) for k in range(bits)]

    barrier = pltpu.get_barrier_semaphore()

    def greet(device):
        pl.semaphore_signal(barrier, inc=1, device_id=device, device_id_type=MESH)

    for peer in rec_peers:
        greet({"rec": peer})
    for d in range(1, peers):
        greet({"query": lax.rem(y + d, peers)})
    greet({"tm": inward})

    @pl.when(jnp.logical_not(is_end))
    def _():
        greet({"tm": outward})

    pl.semaphore_wait(barrier, jnp.where(is_end, bits + peers, bits + peers + 1))

    queries, width = (qu_ref.shape[0], fr_ref.shape[1])
    count = queries // chunk
    cols = width // recs
    fcols = width // peers
    row_count = sg_ref.shape[0]

    def copy(src, dst, send, recv, device):
        return pltpu.make_async_remote_copy(
            src_ref=src,
            dst_ref=dst,
            send_sem=send,
            recv_sem=recv,
            device_id=device,
            device_id_type=MESH,
        )

    def at(c):
        return pl.ds(pl.multiple_of(c * chunk, chunk), chunk)

    def f_copy(d):
        p = lax.rem(y + d, peers)
        return copy(fpart.at[p], fin.at[d - 1], f_send.at[d - 1], f_recv.at[d - 1], {"query": p})

    def f_compute(p):
        tile = 128
        columns = pl.ds(pl.multiple_of(p * fcols, fcols), fcols)

        def body(i, carry):
            rows = pl.ds(pl.multiple_of(i * tile, tile), tile)
            fpart[p, rows, :] = jnp.dot(
                sg_ref[rows, :], qu_ref[:, columns], preferred_element_type=jnp.float32
            )
            return carry

        lax.fori_loop(0, row_count // tile, body, 0)

    def rec_copies(k, c):
        n = recs >> k
        theirs = (1 - my_bits[k]) * (n // 2)
        device = {"rec": rec_peers[k]}
        return (
            copy(
                acc[k].at[pl.ds(theirs, n // 2), at(c)],
                arrived[k].at[:, at(c)],
                rec_send.at[k, 0, c],
                rec_recv.at[k, 0, c],
                device,
            ),
            copy(
                kacc[k].at[c],
                karrived[k].at[c],
                rec_send.at[k, 1, c],
                rec_recv.at[k, 1, c],
                device,
            ),
        )

    def summed(k, c):
        for one in rec_copies(k, c):
            one.wait_recv()
        n = recs >> k
        mine = my_bits[k] * (n // 2)
        total = acc[k][pl.ds(mine, n // 2), at(c), :] + arrived[k][:, at(c), :]
        return total, kacc[k][c] + karrived[k][c]

    def inward_copies(c, to_mid):
        big, small = (inner, kinner) if to_mid else (outer, kouter)
        recv = inn_recv if to_mid else out_recv
        device = {"tm": inward}
        return (
            copy(mid.at[at(c)], big.at[at(c)], in_send.at[0, c], recv.at[0, c], device),
            copy(kmid.at[c], small.at[c], in_send.at[1, c], recv.at[1, c], device),
        )

    def outward_copies(c):
        device = {"tm": outward}
        return (
            copy(inner.at[at(c)], inner.at[at(c)], out_send.at[0, c], inn_recv.at[0, c], device),
            copy(kinner.at[c], kinner.at[c], out_send.at[1, c], inn_recv.at[1, c], device),
        )

    def start(c):
        part = lax.dot_general(
            sg_ref[:, at(c)],
            fr_ref[...],
            (((0,), (0,)), ((), ())),
            preferred_element_type=jnp.float32,
        )
        for p in range(recs):
            j = bit_reversed(p, bits)
            acc[0][p, at(c), :] = part[:, j * cols : (j + 1) * cols]
        kacc[0][c] = kp_ref[:, at(c)]
        for one in rec_copies(0, c):
            one.start()

    def exchange(k, c):
        total, ktotal = summed(k - 1, c)
        acc[k][:, at(c), :] = total
        kacc[k][c] = ktotal
        for one in rec_copies(k, c):
            one.start()

    def gather_in(c):
        total, ktotal = summed(bits - 1, c)
        mid[at(c), :] = total[0]
        kmid[c] = ktotal

        @pl.when(jnp.logical_not(is_end))
        def _():
            for one in inward_copies(c, False):
                one.wait_recv()
            mid[at(c), :] += outer[at(c), :]
            kmid[c] += kouter[c]

        @pl.when(is_mid)
        def _():
            for one in inward_copies(c, True):
                one.start()

        @pl.when(jnp.logical_not(is_mid))
        def _():
            for one in inward_copies(c, False):
                one.start()

    def spread_out(c):
        for one in inward_copies(c, True):
            one.wait_recv()

        @pl.when(is_mid)
        def _():
            inner[at(c), :] += mid[at(c), :]
            kinner[c] += kmid[c]

        @pl.when(jnp.logical_not(is_end))
        def _():
            for one in outward_copies(c):
                one.start()

        gq_ref[at(c), :] = (inner[at(c), :] * scale).astype(gq_ref.dtype)
        gk_ref[:, at(c)] = kinner[c]

    for d in range(1, peers):
        f_compute(lax.rem(y + d, peers))
        f_copy(d).start()

    lag = bits + 4
    stages = [(0, start)]
    stages += [(k, functools.partial(exchange, k)) for k in range(1, bits)]
    stages += [(bits, gather_in), (lag, spread_out)]

    def step(s, carry):
        for delay, stage in stages:
            @pl.when((s >= delay) & (s < count + delay))
            def _(stage=stage, delay=delay):
                stage(s - delay)
        return carry

    lax.fori_loop(0, count + lag, step, 0)

    f_compute(y)
    for d in range(1, peers):
        f_copy(d).wait_recv()
    total = fpart[y]
    for d in range(1, peers):
        total = total + fin[d - 1]
    gf_ref[...] = (total * scale).astype(gf_ref.dtype)
    for d in range(1, peers):
        f_copy(d).wait_send()

    def drain(c, carry):
        for k in range(bits):
            for one in rec_copies(k, c):
                one.wait_send()
        for one in inward_copies(c, False):
            one.wait_send()

        @pl.when(jnp.logical_not(is_end))
        def _():
            for one in outward_copies(c):
                one.wait_send()

        return carry

    lax.fori_loop(0, count, drain, 0)


def gradients(score_grad, frame_rows, queries, kernel_part, scale):
    tms, peers, recs = (lax.axis_size("tm"), lax.axis_size("query"), lax.axis_size("rec"))
    bits = recs.bit_length() - 1
    row_count, width = frame_rows.shape
    query_count = queries.shape[0]
    taps = kernel_part.shape[0]
    chunk = 128
    count = query_count // chunk
    cols, fcols = (width // recs, width // peers)
    f32 = jnp.float32
    small = pltpu.VMEM((count, taps, chunk), f32)
    block = pltpu.VMEM((query_count, cols), f32)
    scratch = [pltpu.VMEM((recs >> k, query_count, cols), f32) for k in range(bits)]
    scratch += [pltpu.VMEM((recs >> (k + 1), query_count, cols), f32) for k in range(bits)]
    scratch += [small] * (2 * bits) + [block] * 3 + [small] * 3
    scratch += [
        pltpu.VMEM((peers, row_count, fcols), f32),
        pltpu.VMEM((peers - 1, row_count, fcols), f32),
    ]
    dma = pltpu.SemaphoreType.DMA
    scratch += [dma((bits, 2, count))] * 2 + [dma((2, count))] * 4 + [dma((peers - 1,))] * 2
    vmem = pl.BlockSpec(memory_space=pltpu.VMEM)
    return pl.pallas_call(
        functools.partial(gradient_kernel, (tms, peers, recs, chunk), scale),
        out_shape=(
            jax.ShapeDtypeStruct((row_count, fcols), jnp.bfloat16),
            jax.ShapeDtypeStruct((query_count, cols), jnp.bfloat16),
            jax.ShapeDtypeStruct((taps, query_count), f32),
        ),
        in_specs=[vmem] * 4,
        out_specs=(vmem,) * 3,
        scratch_shapes=scratch,
        compiler_params=pltpu.CompilerParams(
            collective_id=0, has_side_effects=True, vmem_limit_bytes=60 * 1024 * 1024
        ),
        name="gradients",
    )(score_grad, frame_rows, queries, kernel_part)


def tap_sum(kernel, padded, row_count, flipped):
    tap_count = kernel.shape[0]
    running = jnp.zeros((row_count, padded.shape[1]), jnp.float32)
    for offset in range(tap_count):
        begin_row = tap_count - 1 - offset if flipped else offset
        running = running + kernel[offset][None, :] * padded[begin_row : begin_row + row_count]
    return running


def combine_stats(first_pair, second_pair):
    top_value = jnp.maximum(first_pair[0], second_pair[0])
    total_value = first_pair[1] * jnp.exp(first_pair[0] - top_value) + second_pair[1] * jnp.exp(
        second_pair[0] - top_value
    )
    return jnp.stack([top_value, total_value])


def row_softmax(smooth):
    local_top = jnp.max(smooth, axis=1)
    local_total = jnp.sum(jnp.exp(smooth - local_top[:, None]), axis=1)
    stats = merged(jnp.stack([local_top, local_total]), "query", combine_stats)
    top_value, total_value = stats[0], stats[1]
    return jnp.exp(smooth - top_value[:, None]) / total_value[:, None]


def per_device(frames, queries, kernel, labels, lengths):
    frame_rows = frames[0]
    label_ids = labels[0]
    length_now = lengths[0]
    row_count = frame_rows.shape[0]
    query_count = queries.shape[0]
    width = frame_rows.shape[1]
    tap_count = kernel.shape[0]
    rim_width = tap_count // 2
    logit_scale = 10.0 / math.sqrt(width)
    frame_start = lax.axis_index("tm") * row_count
    is_valid = frame_start + jnp.arange(row_count, dtype=jnp.int32) < length_now
    query_start = lax.axis_index("query") * query_count
    query_ids = query_start + jnp.arange(query_count, dtype=jnp.int32)
    halo = 2 * rim_width
    tagged = jnp.concatenate(
        [
            frame_rows.astype(jnp.float32),
            jnp.broadcast_to(label_ids.astype(jnp.float32)[:, None], (row_count, 128)),
        ],
        axis=1,
    )
    before, after = halo_rows(tagged, "tm", halo)
    rim_rows = jnp.concatenate([before[:, :width], after[:, :width]]).astype(jnp.bfloat16)

    def scored(rows):
        return (
            lax.dot_general(
                rows, queries, (((1,), (1,)), ((), ())), preferred_element_type=jnp.float32
            )
            * logit_scale
        )

    inner = scored(frame_rows)
    rim = scored(rim_rows)
    wide = jnp.concatenate([rim[:halo], inner, rim[halo:]])
    wide_frames = frame_start - halo + jnp.arange(row_count + 2 * halo, dtype=jnp.int32)
    wide_valid = (wide_frames >= 0) & (wide_frames < length_now)
    wide = jnp.where(wide_valid[:, None], wide, 0.0)
    label_pad = jnp.concatenate(
        [
            before[halo - rim_width :, width].astype(jnp.int32),
            label_ids,
            after[:rim_width, width].astype(jnp.int32),
        ]
    )
    ext_rows = row_count + 2 * rim_width
    ext_frames = frame_start - rim_width + jnp.arange(ext_rows, dtype=jnp.int32)
    ext_valid = (ext_frames >= 0) & (ext_frames < length_now)
    smooth = tap_sum(kernel, wide, ext_rows, False)
    softmax_out = row_softmax(smooth)
    positive = (label_pad[:, None] == query_ids[None, :]).astype(jnp.float32)
    grad_pad = jnp.where(ext_valid[:, None], softmax_out - positive, 0.0)
    map_grad = grad_pad[rim_width : rim_width + row_count]
    padded = wide[rim_width : rim_width + row_count + 2 * rim_width]
    score_grad = tap_sum(kernel, grad_pad, row_count, True)
    score_grad = jnp.where(is_valid[:, None], score_grad, 0.0).astype(jnp.bfloat16)
    kernel_part = jnp.stack(
        [
            jnp.sum(map_grad * padded[offset : offset + row_count], axis=0)
            for offset in range(tap_count)
        ]
    )
    grad_frames, grad_queries, grad_kernel = gradients(
        score_grad, frame_rows, queries, kernel_part, logit_scale
    )
    return (grad_frames[None], grad_queries, grad_kernel)


def solution(mesh):
    in_specs = (P("rec", "tm", None), P("query", None), P(None, "query"), P("rec", "tm"), P("rec"))
    out_specs = (P("rec", "tm", "query"), P("query", "rec"), P(None, "query"))
    return jax.shard_map(
        per_device, mesh=mesh, in_specs=in_specs, out_specs=out_specs, check_vma=False
    )
```

```python
import functools
import math

import jax
import jax.numpy as jnp
from jax import lax
from jax.experimental import pallas as pl
from jax.experimental.pallas import tpu as pltpu
from jax.sharding import PartitionSpec as P


def merged(x, axis, combine):
    peers = lax.axis_size(axis)
    step = 1
    while step < peers:
        swap = [(i, i ^ step) for i in range(peers)]
        x = combine(x, lax.ppermute(x, axis, swap))
        step *= 2
    return x


def halo_rows(x, axis, width):
    peers = lax.axis_size(axis)
    up = [(i, i + 1) for i in range(peers - 1)]
    down = [(i + 1, i) for i in range(peers - 1)]
    before = lax.ppermute(x[x.shape[0] - width :], axis, up)
    after = lax.ppermute(x[:width], axis, down)
    return lax.optimization_barrier((before, after))


GROUPS = 4
LANES = 128


def spread_taps(kern_ref, lanes):
    taps = kern_ref.shape[0]
    return [jnp.broadcast_to(kern_ref[j : j + 1, lanes], (8, LANES)) for j in range(taps)]


def tap_block(load, taps, flipped):
    count = len(taps)
    sums = [None] * GROUPS
    for o in range(8 * (GROUPS - 1) + count):
        v = load(o)
        for i in range(GROUPS):
            j = o - 8 * i
            if 0 <= j < count:
                term = taps[count - 1 - j if flipped else j] * v
                sums[i] = term if sums[i] is None else sums[i] + term
    return sums


def smooth_kernel(scale, x_ref, q_ref, kern_ref, valid_ref, sc_ref, e_ref, top_ref, total_ref):
    tiles, ext, _ = e_ref.shape
    wide = x_ref.shape[0]
    pair = 2 * LANES
    block = 8 * GROUPS

    top_ref[...] = jnp.full_like(top_ref, -jnp.inf)

    def score(c, carry):
        rows = pl.ds(pl.multiple_of(c * pair, pair), pair)
        part = lax.dot_general(
            x_ref[...],
            q_ref[rows, :],
            (((1,), (1,)), ((), ())),
            preferred_element_type=jnp.float32,
        )
        for h in range(2):
            one = part[:, h * LANES : (h + 1) * LANES] * scale
            sc_ref[2 * c + h] = jnp.where(valid_ref[...] > 0, one, 0.0)
        return carry

    lax.fori_loop(0, tiles // 2, score, 0)

    def smoothed(c, carry):
        taps = spread_taps(kern_ref, pl.ds(pl.multiple_of(c * LANES, LANES), LANES))

        def body(g, carry):
            base = pl.multiple_of(g * block, block)
            sums = tap_block(lambda o: sc_ref[c, pl.ds(base + o, 8), :], taps, False)
            for i in range(GROUPS):
                rows = pl.ds(base + 8 * i, 8)
                e_ref[c, rows, :] = sums[i]
                top_ref[rows, :] = jnp.maximum(top_ref[rows, :], sums[i])
            return carry

        return lax.fori_loop(0, ext // block, body, carry)

    lax.fori_loop(0, tiles, smoothed, 0)

    def finish(g, carry):
        rows = pl.ds(pl.multiple_of(g * block, block), block)
        top = jnp.max(top_ref[rows, :], axis=1, keepdims=True)
        top = jnp.broadcast_to(top, (block, LANES))
        top_ref[rows, :] = top
        total = jnp.zeros((block, LANES), jnp.float32)
        for c in range(tiles):
            e = jnp.exp(e_ref[c, rows, :] - top)
            e_ref[c, rows, :] = e
            total = total + e
        total = jnp.sum(total, axis=1, keepdims=True)
        total_ref[rows, :] = jnp.broadcast_to(total, (block, LANES))
        return carry

    lax.fori_loop(0, ext // block, finish, 0)


def smooth_exp(rows, queries, kernel, valid, scale):
    wide = rows.shape[0]
    query_count = queries.shape[0]
    ext = wide - (kernel.shape[0] // 2) * 2
    tiles = query_count // LANES
    f32 = jnp.float32
    vmem = pl.BlockSpec(memory_space=pltpu.VMEM)
    return pl.pallas_call(
        functools.partial(smooth_kernel, scale),
        out_shape=(
            jax.ShapeDtypeStruct((tiles, wide, LANES), f32),
            jax.ShapeDtypeStruct((tiles, ext, LANES), f32),
            jax.ShapeDtypeStruct((ext, LANES), f32),
            jax.ShapeDtypeStruct((ext, LANES), f32),
        ),
        in_specs=[vmem] * 4,
        out_specs=(vmem,) * 4,
        compiler_params=pltpu.CompilerParams(vmem_limit_bytes=40 * 1024 * 1024),
        name="smooth",
    )(rows, queries, kernel, valid)


MESH = pl.DeviceIdType.MESH


def bit_reversed(p, bits):
    return sum(((p >> k) & 1) << (bits - 1 - k) for k in range(bits))


def gradient_kernel(
    dims, scale, sc_ref, e_ref, f_ref, lab_ref, fr_ref, qu_ref, kern_ref, gf_ref, gq_ref, gk_ref,
    *scratch,
):
    tms, peers, recs, chunk = dims
    bits = recs.bit_length() - 1
    acc, scratch = scratch[:bits], scratch[bits:]
    arrived, scratch = scratch[:bits], scratch[bits:]
    kacc, scratch = scratch[:bits], scratch[bits:]
    karrived, scratch = scratch[:bits], scratch[bits:]
    (mid, outer, inner, kmid, kouter, kinner, fpart, fin, sg_ref, grad, ksum) = scratch[:11]
    (rec_send, rec_recv, in_send, out_recv, out_send, inn_recv, f_send, f_recv) = scratch[11:]

    t = lax.axis_index("tm")
    y = lax.axis_index("query")
    r = lax.axis_index("rec")
    half = tms // 2
    low = t < half
    is_end = (t == 0) | (t == tms - 1)
    is_mid = (t == half - 1) | (t == half)
    inward = jnp.where(low, t + 1, t - 1)
    outward = jnp.where(low, lax.rem(t + tms - 1, tms), lax.rem(t + 1, tms))
    my_bits = [lax.rem(r // (1 << k), 2) for k in range(bits)]
    rec_peers = [r + (1 - 2 * my_bits[k]) * (1 << k) for k in range(bits)]

    barrier = pltpu.get_barrier_semaphore()

    def greet(device):
        pl.semaphore_signal(barrier, inc=1, device_id=device, device_id_type=MESH)

    for peer in rec_peers:
        greet({"rec": peer})
    for d in range(1, peers):
        greet({"query": lax.rem(y + d, peers)})
    greet({"tm": inward})

    @pl.when(jnp.logical_not(is_end))
    def _():
        greet({"tm": outward})

    pl.semaphore_wait(barrier, jnp.where(is_end, bits + peers, bits + peers + 1))

    queries, width = (qu_ref.shape[0], fr_ref.shape[1])
    count = queries // chunk
    cols = width // recs
    fcols = width // peers
    row_count = sg_ref.shape[0]

    def copy(src, dst, send, recv, device):
        return pltpu.make_async_remote_copy(
            src_ref=src,
            dst_ref=dst,
            send_sem=send,
            recv_sem=recv,
            device_id=device,
            device_id_type=MESH,
        )

    def at(c):
        return pl.ds(pl.multiple_of(c * chunk, chunk), chunk)

    def f_copy(d):
        p = lax.rem(y + d, peers)
        return copy(fpart.at[p], fin.at[d - 1], f_send.at[d - 1], f_recv.at[d - 1], {"query": p})

    def f_compute(p):
        tile = 128
        columns = pl.ds(pl.multiple_of(p * fcols, fcols), fcols)

        def body(i, carry):
            rows = pl.ds(pl.multiple_of(i * tile, tile), tile)
            fpart[p, rows, :] = jnp.dot(
                sg_ref[rows, :], qu_ref[:, columns], preferred_element_type=jnp.float32
            )
            return carry

        lax.fori_loop(0, row_count // tile, body, 0)

    def rec_copies(k, c):
        n = recs >> k
        theirs = (1 - my_bits[k]) * (n // 2)
        device = {"rec": rec_peers[k]}
        return (
            copy(
                acc[k].at[pl.ds(theirs, n // 2), at(c)],
                arrived[k].at[:, at(c)],
                rec_send.at[k, 0, c],
                rec_recv.at[k, 0, c],
                device,
            ),
            copy(
                kacc[k].at[c],
                karrived[k].at[c],
                rec_send.at[k, 1, c],
                rec_recv.at[k, 1, c],
                device,
            ),
        )

    def summed(k, c):
        for one in rec_copies(k, c):
            one.wait_recv()
        n = recs >> k
        mine = my_bits[k] * (n // 2)
        total = acc[k][pl.ds(mine, n // 2), at(c), :] + arrived[k][:, at(c), :]
        return total, kacc[k][c] + karrived[k][c]

    def inward_copies(c, to_mid):
        big, small = (inner, kinner) if to_mid else (outer, kouter)
        recv = inn_recv if to_mid else out_recv
        device = {"tm": inward}
        return (
            copy(mid.at[at(c)], big.at[at(c)], in_send.at[0, c], recv.at[0, c], device),
            copy(kmid.at[c], small.at[c], in_send.at[1, c], recv.at[1, c], device),
        )

    def outward_copies(c):
        device = {"tm": outward}
        return (
            copy(inner.at[at(c)], inner.at[at(c)], out_send.at[0, c], inn_recv.at[0, c], device),
            copy(kinner.at[c], kinner.at[c], out_send.at[1, c], inn_recv.at[1, c], device),
        )

    taps_n = kern_ref.shape[0]
    rim = taps_n // 2
    block = 8 * GROUPS
    ext = grad.shape[0]
    lane = lax.broadcasted_iota(jnp.int32, (8, LANES), 1) + y * queries

    def map_gradient(c):
        first = lane + c * chunk

        def body(g, carry):
            for i in range(GROUPS):
                rows = pl.ds(pl.multiple_of(g * block + 8 * i, 8), 8)
                hit = jnp.where(lab_ref[rows, :] == first, 1.0, 0.0)
                factor = f_ref[rows, :]
                value = e_ref[c, rows, :] * jnp.maximum(factor, 0.0) - hit
                grad[rows, :] = jnp.where(factor >= 0.0, value, 0.0)
            return carry

        lax.fori_loop(0, ext // block, body, 0)

    def score_gradient(c):
        taps = spread_taps(kern_ref, at(c))

        def body(g, carry):
            base = pl.multiple_of(g * block, block)
            sums = tap_block(lambda o: grad[pl.ds(base + o, 8), :], taps, True)
            valid = f_ref[pl.ds(base + rim, block), :] >= 0.0
            total = jnp.where(valid, jnp.concatenate(sums, axis=0), 0.0)
            sg_ref[pl.ds(base, block), at(c)] = total.astype(jnp.bfloat16)
            return carry

        lax.fori_loop(0, row_count // block, body, 0)

    def tap_gradient(c):
        def body(g, sums):
            base = pl.multiple_of(g * block, block)
            held = [grad[pl.ds(base + rim + 8 * i, 8), :] for i in range(GROUPS)]
            sums = list(sums)
            for o in range(8 * (GROUPS - 1) + taps_n):
                v = sc_ref[c, pl.ds(base + rim + o, 8), :]
                for i in range(GROUPS):
                    j = o - 8 * i
                    if 0 <= j < taps_n:
                        sums[j] = sums[j] + held[i] * v
            return tuple(sums)

        zero = jnp.zeros((8, LANES), jnp.float32)
        sums = lax.fori_loop(0, row_count // block, body, (zero,) * taps_n)
        for j in range(taps_n):
            ksum[j : j + 1, :] = jnp.sum(sums[j], axis=0, keepdims=True)

    def start(c):
        map_gradient(c)
        score_gradient(c)
        tap_gradient(c)
        part = lax.dot_general(
            sg_ref[:, at(c)],
            fr_ref[...],
            (((0,), (0,)), ((), ())),
            preferred_element_type=jnp.float32,
        )
        for p in range(recs):
            j = bit_reversed(p, bits)
            acc[0][p, at(c), :] = part[:, j * cols : (j + 1) * cols]
        kacc[0][c] = ksum[...]
        for one in rec_copies(0, c):
            one.start()

    def exchange(k, c):
        total, ktotal = summed(k - 1, c)
        acc[k][:, at(c), :] = total
        kacc[k][c] = ktotal
        for one in rec_copies(k, c):
            one.start()

    def gather_in(c):
        total, ktotal = summed(bits - 1, c)
        mid[at(c), :] = total[0]
        kmid[c] = ktotal

        @pl.when(jnp.logical_not(is_end))
        def _():
            for one in inward_copies(c, False):
                one.wait_recv()
            mid[at(c), :] += outer[at(c), :]
            kmid[c] += kouter[c]

        @pl.when(is_mid)
        def _():
            for one in inward_copies(c, True):
                one.start()

        @pl.when(jnp.logical_not(is_mid))
        def _():
            for one in inward_copies(c, False):
                one.start()

    def spread_out(c):
        for one in inward_copies(c, True):
            one.wait_recv()

        @pl.when(is_mid)
        def _():
            inner[at(c), :] += mid[at(c), :]
            kinner[c] += kmid[c]

        @pl.when(jnp.logical_not(is_end))
        def _():
            for one in outward_copies(c):
                one.start()

        gq_ref[at(c), :] = (inner[at(c), :] * scale).astype(gq_ref.dtype)
        gk_ref[:, at(c)] = kinner[c]

    def send_frames():
        for d in range(1, peers):
            f_compute(lax.rem(y + d, peers))
            f_copy(d).start()

    reach = half - 1
    away = jnp.where(low, reach - t, t - half)
    in_lag = bits + 1 + 2 * (reach - away)
    out_lag = bits + 3 + 2 * (reach + away)
    last_lag = bits + 3 + 4 * reach
    stages = [(0, start), (out_lag, spread_out), (in_lag, gather_in)]
    stages += [(k, functools.partial(exchange, k)) for k in range(bits - 1, 0, -1)]

    def step(s, carry):
        @pl.when(s == count)
        def _():
            send_frames()

        for delay, stage in stages:
            @pl.when((s >= delay) & (s < count + delay))
            def _(stage=stage, delay=delay):
                stage(s - delay)
        return carry

    lax.fori_loop(0, count + last_lag, step, 0)

    f_compute(y)
    for d in range(1, peers):
        f_copy(d).wait_recv()
    total = fpart[y]
    for d in range(1, peers):
        total = total + fin[d - 1]
    gf_ref[...] = (total * scale).astype(gf_ref.dtype)
    for d in range(1, peers):
        f_copy(d).wait_send()

    def drain(c, carry):
        for k in range(bits):
            for one in rec_copies(k, c):
                one.wait_send()
        for one in inward_copies(c, False):
            one.wait_send()

        @pl.when(jnp.logical_not(is_end))
        def _():
            for one in outward_copies(c):
                one.wait_send()

        return carry

    lax.fori_loop(0, count, drain, 0)


def gradients(scores, exps, factor, labels, frame_rows, queries, kernel, scale):
    tms, peers, recs = (lax.axis_size("tm"), lax.axis_size("query"), lax.axis_size("rec"))
    bits = recs.bit_length() - 1
    row_count, width = frame_rows.shape
    query_count = queries.shape[0]
    taps = kernel.shape[0]
    chunk = LANES
    count = query_count // chunk
    cols, fcols = (width // recs, width // peers)
    f32 = jnp.float32
    small = pltpu.VMEM((count, taps, chunk), f32)
    block = pltpu.VMEM((query_count, cols), f32)
    scratch = [pltpu.VMEM((recs >> k, query_count, cols), f32) for k in range(bits)]
    scratch += [pltpu.VMEM((recs >> (k + 1), query_count, cols), f32) for k in range(bits)]
    scratch += [small] * (2 * bits) + [block] * 3 + [small] * 3
    scratch += [
        pltpu.VMEM((peers, row_count, fcols), f32),
        pltpu.VMEM((peers - 1, row_count, fcols), f32),
        pltpu.VMEM((row_count, query_count), jnp.bfloat16),
        pltpu.VMEM((exps.shape[1], chunk), f32),
        pltpu.VMEM((taps, chunk), f32),
    ]
    dma = pltpu.SemaphoreType.DMA
    scratch += [dma((bits, 2, count))] * 2 + [dma((2, count))] * 4 + [dma((peers - 1,))] * 2
    vmem = pl.BlockSpec(memory_space=pltpu.VMEM)
    return pl.pallas_call(
        functools.partial(gradient_kernel, (tms, peers, recs, chunk), scale),
        out_shape=(
            jax.ShapeDtypeStruct((row_count, fcols), jnp.bfloat16),
            jax.ShapeDtypeStruct((query_count, cols), jnp.bfloat16),
            jax.ShapeDtypeStruct((taps, query_count), f32),
        ),
        in_specs=[vmem] * 7,
        out_specs=(vmem,) * 3,
        scratch_shapes=scratch,
        compiler_params=pltpu.CompilerParams(
            collective_id=0, has_side_effects=True, vmem_limit_bytes=60 * 1024 * 1024
        ),
        name="gradients",
    )(scores, exps, factor, labels, frame_rows, queries, kernel)


def combine_stats(first_pair, second_pair):
    top_value = jnp.maximum(first_pair[0], second_pair[0])
    total_value = first_pair[1] * jnp.exp(first_pair[0] - top_value) + second_pair[1] * jnp.exp(
        second_pair[0] - top_value
    )
    return jnp.stack([top_value, total_value])


def per_device(frames, queries, kernel, labels, lengths):
    frame_rows = frames[0]
    label_ids = labels[0]
    length_now = lengths[0]
    row_count = frame_rows.shape[0]
    query_count = queries.shape[0]
    width = frame_rows.shape[1]
    tap_count = kernel.shape[0]
    rim_width = tap_count // 2
    logit_scale = 10.0 / math.sqrt(width)
    frame_start = lax.axis_index("tm") * row_count
    halo = 2 * rim_width
    tagged = jnp.concatenate(
        [
            frame_rows.astype(jnp.float32),
            jnp.broadcast_to(label_ids.astype(jnp.float32)[:, None], (row_count, 128)),
        ],
        axis=1,
    )
    before, after = halo_rows(tagged, "tm", halo)
    rim_rows = jnp.concatenate([before[:, :width], after[:, :width]]).astype(jnp.bfloat16)

    wide_rows = jnp.concatenate([rim_rows[:halo], frame_rows, rim_rows[halo:]])
    wide_frames = frame_start - halo + jnp.arange(row_count + 2 * halo, dtype=jnp.int32)
    wide_valid = (wide_frames >= 0) & (wide_frames < length_now)
    wide_valid = jnp.broadcast_to(wide_valid[:, None], (wide_valid.shape[0], LANES))
    label_pad = jnp.concatenate(
        [
            before[halo - rim_width :, width].astype(jnp.int32),
            label_ids,
            after[:rim_width, width].astype(jnp.int32),
        ]
    )
    ext_rows = row_count + 2 * rim_width
    ext_frames = frame_start - rim_width + jnp.arange(ext_rows, dtype=jnp.int32)
    ext_valid = (ext_frames >= 0) & (ext_frames < length_now)
    scores, exps, local_top, local_total = smooth_exp(
        wide_rows, queries, kernel, wide_valid.astype(jnp.float32), logit_scale
    )
    top = local_top[:, 0]
    stats = merged(jnp.stack([top, local_total[:, 0]]), "query", combine_stats)
    factor = jnp.exp(top - stats[0]) / stats[1]
    factor = jnp.where(ext_valid, factor, -1.0)
    factor = jnp.broadcast_to(factor[:, None], (ext_rows, LANES))
    label_wide = jnp.broadcast_to(label_pad[:, None], (ext_rows, LANES))
    grad_frames, grad_queries, grad_kernel = gradients(
        scores, exps, factor, label_wide, frame_rows, queries, kernel, logit_scale
    )
    return (grad_frames[None], grad_queries, grad_kernel)


def solution(mesh):
    in_specs = (P("rec", "tm", None), P("query", None), P(None, "query"), P("rec", "tm"), P("rec"))
    out_specs = (P("rec", "tm", "query"), P("query", "rec"), P(None, "query"))
    return jax.shard_map(
        per_device, mesh=mesh, in_specs=in_specs, out_specs=out_specs, check_vma=False
    )
```

```python
import functools
import math

import jax
import jax.numpy as jnp
from jax import lax
from jax.experimental import pallas as pl
from jax.experimental.pallas import tpu as pltpu
from jax.sharding import PartitionSpec as P


GROUPS = 4
LANES = 128


def spread_taps(kern_ref, lanes):
    taps = kern_ref.shape[0]
    return [jnp.broadcast_to(kern_ref[j : j + 1, lanes], (8, LANES)) for j in range(taps)]


def tap_block(load, taps, flipped):
    count = len(taps)
    sums = [None] * GROUPS
    for o in range(8 * (GROUPS - 1) + count):
        v = load(o)
        for i in range(GROUPS):
            j = o - 8 * i
            if 0 <= j < count:
                term = taps[count - 1 - j if flipped else j] * v
                sums[i] = term if sums[i] is None else sums[i] + term
    return sums


MESH = pl.DeviceIdType.MESH


def bit_reversed(p, bits):
    return sum(((p >> k) & 1) << (bits - 1 - k) for k in range(bits))


def gradient_kernel(
    dims,
    scale,
    halo_ref,
    own_lab_ref,
    len_ref,
    fr_ref,
    qu_ref,
    kern_ref,
    gf_ref,
    gq_ref,
    gk_ref,
    *scratch,
):
    tms, peers, recs, chunk = dims
    bits = recs.bit_length() - 1
    acc, scratch = scratch[:bits], scratch[bits:]
    arrived, scratch = scratch[:bits], scratch[bits:]
    kacc, scratch = scratch[:bits], scratch[bits:]
    karrived, scratch = scratch[:bits], scratch[bits:]
    (mid, outer, inner, kmid, kouter, kinner, fpart, fin, sg_ref, grad, ksum) = scratch[:11]
    (sc_ref, e_ref, f_ref, lab_ref, valid_ref, x_ref, hin, stat, stat_in) = scratch[11:20]
    scratch = scratch[20:]
    (rec_send, rec_recv, in_send, out_recv, out_send, inn_recv, f_send, f_recv) = scratch[:8]
    (h_send, h_recv, s_send, s_recv) = scratch[8:]

    t = lax.axis_index("tm")
    y = lax.axis_index("query")
    r = lax.axis_index("rec")
    half = tms // 2
    low = t < half
    is_end = (t == 0) | (t == tms - 1)
    is_mid = (t == half - 1) | (t == half)
    inward = jnp.where(low, t + 1, t - 1)
    outward = jnp.where(low, lax.rem(t + tms - 1, tms), lax.rem(t + 1, tms))
    my_bits = [lax.rem(r // (1 << k), 2) for k in range(bits)]
    rec_peers = [r + (1 - 2 * my_bits[k]) * (1 << k) for k in range(bits)]

    barrier = pltpu.get_barrier_semaphore()

    def greet(device):
        pl.semaphore_signal(barrier, inc=1, device_id=device, device_id_type=MESH)

    for peer in rec_peers:
        greet({"rec": peer})
    for d in range(1, peers):
        greet({"query": lax.rem(y + d, peers)})
    greet({"tm": inward})

    @pl.when(jnp.logical_not(is_end))
    def _():
        greet({"tm": outward})

    pl.semaphore_wait(barrier, jnp.where(is_end, bits + peers, bits + peers + 1))

    queries, width = (qu_ref.shape[0], fr_ref.shape[1])
    count = queries // chunk
    cols = width // recs
    fcols = width // peers
    row_count = sg_ref.shape[0]

    def copy(src, dst, send, recv, device):
        return pltpu.make_async_remote_copy(
            src_ref=src,
            dst_ref=dst,
            send_sem=send,
            recv_sem=recv,
            device_id=device,
            device_id_type=MESH,
        )

    def at(c):
        return pl.ds(pl.multiple_of(c * chunk, chunk), chunk)

    def f_copy(d):
        p = lax.rem(y + d, peers)
        return copy(fpart.at[p], fin.at[d - 1], f_send.at[d - 1], f_recv.at[d - 1], {"query": p})

    def f_compute(p):
        tile = 128
        columns = pl.ds(pl.multiple_of(p * fcols, fcols), fcols)

        def body(i, carry):
            rows = pl.ds(pl.multiple_of(i * tile, tile), tile)
            fpart[p, rows, :] = jnp.dot(
                sg_ref[rows, :], qu_ref[:, columns], preferred_element_type=jnp.float32
            )
            return carry

        lax.fori_loop(0, row_count // tile, body, 0)

    def rec_copies(k, c):
        n = recs >> k
        theirs = (1 - my_bits[k]) * (n // 2)
        device = {"rec": rec_peers[k]}
        return (
            copy(
                acc[k].at[pl.ds(theirs, n // 2), at(c)],
                arrived[k].at[:, at(c)],
                rec_send.at[k, 0, c],
                rec_recv.at[k, 0, c],
                device,
            ),
            copy(
                kacc[k].at[c],
                karrived[k].at[c],
                rec_send.at[k, 1, c],
                rec_recv.at[k, 1, c],
                device,
            ),
        )

    def summed(k, c):
        for one in rec_copies(k, c):
            one.wait_recv()
        n = recs >> k
        mine = my_bits[k] * (n // 2)
        total = acc[k][pl.ds(mine, n // 2), at(c), :] + arrived[k][:, at(c), :]
        return total, kacc[k][c] + karrived[k][c]

    def inward_copies(c, to_mid):
        big, small = (inner, kinner) if to_mid else (outer, kouter)
        recv = inn_recv if to_mid else out_recv
        device = {"tm": inward}
        return (
            copy(mid.at[at(c)], big.at[at(c)], in_send.at[0, c], recv.at[0, c], device),
            copy(kmid.at[c], small.at[c], in_send.at[1, c], recv.at[1, c], device),
        )

    def outward_copies(c):
        device = {"tm": outward}
        return (
            copy(inner.at[at(c)], inner.at[at(c)], out_send.at[0, c], inn_recv.at[0, c], device),
            copy(kinner.at[c], kinner.at[c], out_send.at[1, c], inn_recv.at[1, c], device),
        )

    taps_n = kern_ref.shape[0]
    rim = taps_n // 2
    halo = 2 * rim
    block = 8 * GROUPS
    ext = grad.shape[0]
    tiles = e_ref.shape[0]
    wide = x_ref.shape[0]
    lane = lax.broadcasted_iota(jnp.int32, (8, LANES), 1) + y * queries

    def halo_copy(side):
        device = {"tm": lax.rem(t + (tms - 1 if side == 0 else 1), tms)}
        return copy(
            halo_ref.at[side], hin.at[1 - side], h_send.at[side], h_recv.at[1 - side], device
        )

    has = [t > 0, t < tms - 1]
    for side in range(2):
        @pl.when(has[side])
        def _(side=side):
            halo_copy(side).start()

    frame = lax.broadcasted_iota(jnp.int32, (wide, LANES), 0) + (t * row_count - halo)
    valid_ref[...] = jnp.where((frame >= 0) & (frame < len_ref[0]), 1.0, 0.0)
    x_ref[halo : halo + row_count, :] = fr_ref[...]
    lab_ref[rim : rim + row_count, :] = own_lab_ref[...]
    stat[...] = jnp.zeros_like(stat)
    f_ref[...] = jnp.full_like(f_ref, -jnp.inf)

    for side in range(2):
        @pl.when(has[side])
        def _(side=side):
            halo_copy(1 - side).wait_recv()

        @pl.when(jnp.logical_not(has[side]))
        def _(side=side):
            hin[side] = jnp.zeros((halo, hin.shape[2]), jnp.float32)

    x_ref[:halo, :] = hin[0, :, :width].astype(jnp.bfloat16)
    x_ref[halo + row_count :, :] = hin[1, :, :width].astype(jnp.bfloat16)
    lab_ref[:rim, :] = hin[0, halo - rim :, width:]
    lab_ref[rim + row_count :, :] = hin[1, :rim, width:]

    def score(c, carry):
        rows = pl.ds(pl.multiple_of(c * 2 * LANES, 2 * LANES), 2 * LANES)
        part = lax.dot_general(
            x_ref[...],
            qu_ref[rows, :],
            (((1,), (1,)), ((), ())),
            preferred_element_type=jnp.float32,
        )
        for h in range(2):
            one = part[:, h * LANES : (h + 1) * LANES] * scale
            sc_ref[2 * c + h] = jnp.where(valid_ref[...] > 0, one, 0.0)
        return carry

    lax.fori_loop(0, tiles // 2, score, 0)

    def smoothed(c, carry):
        taps = spread_taps(kern_ref, at(c))

        def body(g, carry):
            base = pl.multiple_of(g * block, block)
            sums = tap_block(lambda o: sc_ref[c, pl.ds(base + o, 8), :], taps, False)
            for i in range(GROUPS):
                rows = pl.ds(base + 8 * i, 8)
                e_ref[c, rows, :] = sums[i]
                f_ref[rows, :] = jnp.maximum(f_ref[rows, :], sums[i])
            return carry

        return lax.fori_loop(0, ext // block, body, carry)

    lax.fori_loop(0, tiles, smoothed, 0)

    diagonal = lax.broadcasted_iota(jnp.int32, (block, LANES), 0) == lax.broadcasted_iota(
        jnp.int32, (block, LANES), 1
    )

    def finish(g, carry):
        rows = pl.ds(pl.multiple_of(g * block, block), block)
        top = jnp.max(f_ref[rows, :], axis=1, keepdims=True)
        top = jnp.broadcast_to(top, (block, LANES))
        total = jnp.zeros((block, LANES), jnp.float32)
        for c in range(tiles):
            e = jnp.exp(e_ref[c, rows, :] - top)
            e_ref[c, rows, :] = e
            total = total + e
        total = jnp.broadcast_to(jnp.sum(total, axis=1, keepdims=True), (block, LANES))
        for i, value in enumerate((top, total)):
            picked = jnp.where(diagonal, value, 0.0)
            stat[0, i, pl.ds(g, 1), :] = jnp.sum(picked, axis=0, keepdims=True)
        return carry

    lax.fori_loop(0, ext // block, finish, 0)

    def stat_copy(k):
        bit = lax.rem(y // (1 << k), 2)
        device = {"query": y + (1 - 2 * bit) * (1 << k)}
        return copy(stat.at[k], stat_in.at[k], s_send.at[k], s_recv.at[k], device)

    rounds = peers.bit_length() - 1
    for k in range(rounds):
        stat_copy(k).start()
        stat_copy(k).wait_recv()
        top = jnp.maximum(stat[k, 0], stat_in[k, 0])
        stat[k + 1, 0] = top
        stat[k + 1, 1] = stat[k, 1] * jnp.exp(stat[k, 0] - top) + stat_in[k, 1] * jnp.exp(
            stat_in[k, 0] - top
        )
    stat[rounds, 1] = jnp.exp(stat[0, 0] - stat[rounds, 0]) / stat[rounds, 1]

    def widen(g, carry):
        rows = pl.ds(pl.multiple_of(g * block, block), block)
        row = jnp.broadcast_to(stat[rounds, 1, pl.ds(g, 1), :], (block, LANES))
        factor = jnp.sum(jnp.where(diagonal, row, 0.0), axis=1, keepdims=True)
        factor = jnp.broadcast_to(factor, (block, LANES))
        valid = valid_ref[pl.ds(pl.multiple_of(g * block, block) + rim, block), :] > 0
        f_ref[rows, :] = jnp.where(valid, factor, -1.0)
        return carry

    lax.fori_loop(0, ext // block, widen, 0)

    def map_gradient(c):
        first = (lane + c * chunk).astype(jnp.float32)

        def body(g, carry):
            for i in range(GROUPS):
                rows = pl.ds(pl.multiple_of(g * block + 8 * i, 8), 8)
                hit = jnp.where(lab_ref[rows, :] == first, 1.0, 0.0)
                factor = f_ref[rows, :]
                value = e_ref[c, rows, :] * jnp.maximum(factor, 0.0) - hit
                grad[rows, :] = jnp.where(factor >= 0.0, value, 0.0)
            return carry

        lax.fori_loop(0, ext // block, body, 0)

    def score_gradient(c):
        taps = spread_taps(kern_ref, at(c))

        def body(g, carry):
            base = pl.multiple_of(g * block, block)
            sums = tap_block(lambda o: grad[pl.ds(base + o, 8), :], taps, True)
            valid = f_ref[pl.ds(base + rim, block), :] >= 0.0
            total = jnp.where(valid, jnp.concatenate(sums, axis=0), 0.0)
            sg_ref[pl.ds(base, block), at(c)] = total.astype(jnp.bfloat16)
            return carry

        lax.fori_loop(0, row_count // block, body, 0)

    def tap_gradient(c):
        def body(g, sums):
            base = pl.multiple_of(g * block, block)
            held = [grad[pl.ds(base + rim + 8 * i, 8), :] for i in range(GROUPS)]
            sums = list(sums)
            for o in range(8 * (GROUPS - 1) + taps_n):
                v = sc_ref[c, pl.ds(base + rim + o, 8), :]
                for i in range(GROUPS):
                    j = o - 8 * i
                    if 0 <= j < taps_n:
                        sums[j] = sums[j] + held[i] * v
            return tuple(sums)

        zero = jnp.zeros((8, LANES), jnp.float32)
        sums = lax.fori_loop(0, row_count // block, body, (zero,) * taps_n)
        for j in range(taps_n):
            ksum[j : j + 1, :] = jnp.sum(sums[j], axis=0, keepdims=True)

    def start(c):
        map_gradient(c)
        score_gradient(c)
        tap_gradient(c)
        part = lax.dot_general(
            sg_ref[:, at(c)],
            fr_ref[...],
            (((0,), (0,)), ((), ())),
            preferred_element_type=jnp.float32,
        )
        for p in range(recs):
            j = bit_reversed(p, bits)
            acc[0][p, at(c), :] = part[:, j * cols : (j + 1) * cols]
        kacc[0][c] = ksum[...]
        for one in rec_copies(0, c):
            one.start()

    def exchange(k, c):
        total, ktotal = summed(k - 1, c)
        acc[k][:, at(c), :] = total
        kacc[k][c] = ktotal
        for one in rec_copies(k, c):
            one.start()

    def gather_in(c):
        total, ktotal = summed(bits - 1, c)
        mid[at(c), :] = total[0]
        kmid[c] = ktotal

        @pl.when(jnp.logical_not(is_end))
        def _():
            for one in inward_copies(c, False):
                one.wait_recv()
            mid[at(c), :] += outer[at(c), :]
            kmid[c] += kouter[c]

        @pl.when(is_mid)
        def _():
            for one in inward_copies(c, True):
                one.start()

        @pl.when(jnp.logical_not(is_mid))
        def _():
            for one in inward_copies(c, False):
                one.start()

    def spread_out(c):
        for one in inward_copies(c, True):
            one.wait_recv()

        @pl.when(is_mid)
        def _():
            inner[at(c), :] += mid[at(c), :]
            kinner[c] += kmid[c]

        @pl.when(jnp.logical_not(is_end))
        def _():
            for one in outward_copies(c):
                one.start()

        gq_ref[at(c), :] = (inner[at(c), :] * scale).astype(gq_ref.dtype)
        gk_ref[:, at(c)] = kinner[c]

    def send_frames():
        for d in range(1, peers):
            f_compute(lax.rem(y + d, peers))
            f_copy(d).start()

    reach = half - 1
    away = jnp.where(low, reach - t, t - half)
    in_lag = bits + 1 + 2 * (reach - away)
    out_lag = bits + 3 + 2 * (reach + away)
    last_lag = bits + 3 + 4 * reach
    stages = [(0, start), (out_lag, spread_out), (in_lag, gather_in)]
    stages += [(k, functools.partial(exchange, k)) for k in range(bits - 1, 0, -1)]

    def step(s, carry):
        for delay, stage in stages:
            @pl.when((s >= delay) & (s < count + delay))
            def _(stage=stage, delay=delay):
                stage(s - delay)

        @pl.when(s == count - 1)
        def _():
            send_frames()

        @pl.when(s == count + 1)
        def _():
            f_compute(y)

        return carry

    lax.fori_loop(0, count + last_lag, step, 0)

    for d in range(1, peers):
        f_copy(d).wait_recv()
    total = fpart[y]
    for d in range(1, peers):
        total = total + fin[d - 1]
    gf_ref[...] = (total * scale).astype(gf_ref.dtype)
    for d in range(1, peers):
        f_copy(d).wait_send()

    def drain(c, carry):
        for k in range(bits):
            for one in rec_copies(k, c):
                one.wait_send()
        for one in inward_copies(c, False):
            one.wait_send()

        @pl.when(jnp.logical_not(is_end))
        def _():
            for one in outward_copies(c):
                one.wait_send()

        return carry

    lax.fori_loop(0, count, drain, 0)
    for k in range(rounds):
        stat_copy(k).wait_send()
    for side in range(2):
        @pl.when(has[side])
        def _(side=side):
            halo_copy(side).wait_send()


def gradients(halo_rows, labels, lengths, frame_rows, queries, kernel, scale):
    tms, peers, recs = (lax.axis_size("tm"), lax.axis_size("query"), lax.axis_size("rec"))
    bits = recs.bit_length() - 1
    row_count, width = frame_rows.shape
    query_count = queries.shape[0]
    taps = kernel.shape[0]
    chunk = LANES
    count = query_count // chunk
    cols, fcols = (width // recs, width // peers)
    rim = taps // 2
    ext, wide = (row_count + 2 * rim, row_count + 4 * rim)
    rounds = peers.bit_length() - 1
    stat_rows = (ext // (8 * GROUPS) + 7) // 8 * 8
    f32 = jnp.float32
    small = pltpu.VMEM((count, taps, chunk), f32)
    block = pltpu.VMEM((query_count, cols), f32)
    scratch = [pltpu.VMEM((recs >> k, query_count, cols), f32) for k in range(bits)]
    scratch += [pltpu.VMEM((recs >> (k + 1), query_count, cols), f32) for k in range(bits)]
    scratch += [small] * (2 * bits) + [block] * 3 + [small] * 3
    scratch += [
        pltpu.VMEM((peers, row_count, fcols), f32),
        pltpu.VMEM((peers - 1, row_count, fcols), f32),
        pltpu.VMEM((row_count, query_count), jnp.bfloat16),
        pltpu.VMEM((ext, chunk), f32),
        pltpu.VMEM((taps, chunk), f32),
        pltpu.VMEM((count, wide, chunk), f32),
        pltpu.VMEM((count, ext, chunk), f32),
        pltpu.VMEM((ext, chunk), f32),
        pltpu.VMEM((ext, chunk), f32),
        pltpu.VMEM((wide, chunk), f32),
        pltpu.VMEM((wide, width), jnp.bfloat16),
        pltpu.VMEM(halo_rows.shape, f32),
        pltpu.VMEM((rounds + 1, 2, stat_rows, LANES), f32),
        pltpu.VMEM((rounds, 2, stat_rows, LANES), f32),
    ]
    dma = pltpu.SemaphoreType.DMA
    scratch += [dma((bits, 2, count))] * 2 + [dma((2, count))] * 4 + [dma((peers - 1,))] * 2
    scratch += [dma((2,))] * 2 + [dma((rounds,))] * 2
    vmem = pl.BlockSpec(memory_space=pltpu.VMEM)
    return pl.pallas_call(
        functools.partial(gradient_kernel, (tms, peers, recs, chunk), scale),
        out_shape=(
            jax.ShapeDtypeStruct((row_count, fcols), jnp.bfloat16),
            jax.ShapeDtypeStruct((query_count, cols), jnp.bfloat16),
            jax.ShapeDtypeStruct((taps, query_count), f32),
        ),
        in_specs=[vmem, vmem, pl.BlockSpec(memory_space=pltpu.SMEM), vmem, vmem, vmem],
        out_specs=(vmem,) * 3,
        scratch_shapes=scratch,
        compiler_params=pltpu.CompilerParams(
            collective_id=0, has_side_effects=True, vmem_limit_bytes=60 * 1024 * 1024
        ),
        name="gradients",
    )(halo_rows, labels, lengths, frame_rows, queries, kernel)


def per_device(frames, queries, kernel, labels, lengths):
    frame_rows = frames[0]
    row_count, width = frame_rows.shape
    halo = kernel.shape[0] // 2 * 2
    logit_scale = 10.0 / math.sqrt(width)
    label_wide = jnp.broadcast_to(labels[0].astype(jnp.float32)[:, None], (row_count, LANES))
    ends = (slice(0, halo), slice(row_count - halo, row_count))
    halo_rows = jnp.stack(
        [
            jnp.concatenate([frame_rows[rows].astype(jnp.float32), label_wide[rows]], axis=1)
            for rows in ends
        ]
    )
    grad_frames, grad_queries, grad_kernel = gradients(
        halo_rows, label_wide, lengths, frame_rows, queries, kernel, logit_scale
    )
    return (grad_frames[None], grad_queries, grad_kernel)


def solution(mesh):
    in_specs = (P("rec", "tm", None), P("query", None), P(None, "query"), P("rec", "tm"), P("rec"))
    out_specs = (P("rec", "tm", "query"), P("query", "rec"), P(None, "query"))
    return jax.shard_map(
        per_device, mesh=mesh, in_specs=in_specs, out_specs=out_specs, check_vma=False
    )
```

```python
import functools
import math

import jax
import jax.numpy as jnp
from jax import lax
from jax.experimental import pallas as pl
from jax.experimental.pallas import tpu as pltpu
from jax.sharding import PartitionSpec as P


GROUPS = 4
LANES = 128


def spread_taps(kern_ref, lanes):
    taps = kern_ref.shape[0]
    return [jnp.broadcast_to(kern_ref[j : j + 1, lanes], (8, LANES)) for j in range(taps)]


def tap_block(load, taps, flipped):
    count = len(taps)
    sums = [None] * GROUPS
    for o in range(8 * (GROUPS - 1) + count):
        v = load(o)
        for i in range(GROUPS):
            j = o - 8 * i
            if 0 <= j < count:
                term = taps[count - 1 - j if flipped else j] * v
                sums[i] = term if sums[i] is None else sums[i] + term
    return sums


MESH = pl.DeviceIdType.MESH


def bit_reversed(p, bits):
    return sum(((p >> k) & 1) << (bits - 1 - k) for k in range(bits))


def gradient_kernel(
    dims,
    scale,
    own_lab_ref,
    len_ref,
    fr_ref,
    qu_ref,
    kern_ref,
    gf_ref,
    gq_ref,
    gk_ref,
    *scratch,
):
    tms, peers, recs, chunk = dims
    bits = recs.bit_length() - 1
    acc, scratch = scratch[:bits], scratch[bits:]
    arrived, scratch = scratch[:bits], scratch[bits:]
    kacc, scratch = scratch[:bits], scratch[bits:]
    karrived, scratch = scratch[:bits], scratch[bits:]
    (mid, outer, inner, kmid, kouter, kinner, fpart, fin, sg_ref, grad, ksum) = scratch[:11]
    (sc_ref, e_ref, f_ref, lab_ref, valid_ref, x_ref, hin, hout, stat, stat_in) = scratch[11:21]
    scratch = scratch[21:]
    (rec_send, rec_recv, in_send, out_recv, out_send, inn_recv, f_send, f_recv) = scratch[:8]
    (h_send, h_recv, s_send, s_recv) = scratch[8:]

    t = lax.axis_index("tm")
    y = lax.axis_index("query")
    r = lax.axis_index("rec")
    half = tms // 2
    low = t < half
    is_end = (t == 0) | (t == tms - 1)
    is_mid = (t == half - 1) | (t == half)
    inward = jnp.where(low, t + 1, t - 1)
    outward = jnp.where(low, lax.rem(t + tms - 1, tms), lax.rem(t + 1, tms))
    my_bits = [lax.rem(r // (1 << k), 2) for k in range(bits)]
    rec_peers = [r + (1 - 2 * my_bits[k]) * (1 << k) for k in range(bits)]

    barrier = pltpu.get_barrier_semaphore()

    def greet(device):
        pl.semaphore_signal(barrier, inc=1, device_id=device, device_id_type=MESH)

    for peer in rec_peers:
        greet({"rec": peer})
    for d in range(1, peers):
        greet({"query": lax.rem(y + d, peers)})
    greet({"tm": inward})

    @pl.when(jnp.logical_not(is_end))
    def _():
        greet({"tm": outward})

    pl.semaphore_wait(barrier, jnp.where(is_end, bits + peers, bits + peers + 1))

    queries, width = (qu_ref.shape[0], fr_ref.shape[1])
    count = queries // chunk
    cols = width // recs
    fcols = width // peers
    row_count = sg_ref.shape[0]

    def copy(src, dst, send, recv, device):
        return pltpu.make_async_remote_copy(
            src_ref=src,
            dst_ref=dst,
            send_sem=send,
            recv_sem=recv,
            device_id=device,
            device_id_type=MESH,
        )

    def at(c):
        return pl.ds(pl.multiple_of(c * chunk, chunk), chunk)

    def f_copy(d):
        p = lax.rem(y + d, peers)
        return copy(fpart.at[p], fin.at[d - 1], f_send.at[d - 1], f_recv.at[d - 1], {"query": p})

    def f_compute(p):
        tile = 128
        columns = pl.ds(pl.multiple_of(p * fcols, fcols), fcols)

        def body(i, carry):
            rows = pl.ds(pl.multiple_of(i * tile, tile), tile)
            fpart[p, rows, :] = jnp.dot(
                sg_ref[rows, :], qu_ref[:, columns], preferred_element_type=jnp.float32
            )
            return carry

        lax.fori_loop(0, row_count // tile, body, 0)

    def rec_copies(k, c):
        n = recs >> k
        theirs = (1 - my_bits[k]) * (n // 2)
        device = {"rec": rec_peers[k]}
        return (
            copy(
                acc[k].at[pl.ds(theirs, n // 2), at(c)],
                arrived[k].at[:, at(c)],
                rec_send.at[k, 0, c],
                rec_recv.at[k, 0, c],
                device,
            ),
            copy(
                kacc[k].at[c],
                karrived[k].at[c],
                rec_send.at[k, 1, c],
                rec_recv.at[k, 1, c],
                device,
            ),
        )

    def summed(k, c):
        for one in rec_copies(k, c):
            one.wait_recv()
        n = recs >> k
        mine = my_bits[k] * (n // 2)
        total = acc[k][pl.ds(mine, n // 2), at(c), :] + arrived[k][:, at(c), :]
        return total, kacc[k][c] + karrived[k][c]

    def inward_copies(c, to_mid):
        big, small = (inner, kinner) if to_mid else (outer, kouter)
        recv = inn_recv if to_mid else out_recv
        device = {"tm": inward}
        return (
            copy(mid.at[at(c)], big.at[at(c)], in_send.at[0, c], recv.at[0, c], device),
            copy(kmid.at[c], small.at[c], in_send.at[1, c], recv.at[1, c], device),
        )

    def outward_copies(c):
        device = {"tm": outward}
        return (
            copy(inner.at[at(c)], inner.at[at(c)], out_send.at[0, c], inn_recv.at[0, c], device),
            copy(kinner.at[c], kinner.at[c], out_send.at[1, c], inn_recv.at[1, c], device),
        )

    taps_n = kern_ref.shape[0]
    rim = taps_n // 2
    halo = 2 * rim
    block = 8 * GROUPS
    ext = grad.shape[0]
    tiles = e_ref.shape[0]
    wide = x_ref.shape[0]
    lane = lax.broadcasted_iota(jnp.int32, (8, LANES), 1) + y * queries

    def halo_copy(side):
        device = {"tm": lax.rem(t + (tms - 1 if side == 0 else 1), tms)}
        return copy(
            hout.at[side], hin.at[1 - side], h_send.at[side], h_recv.at[1 - side], device
        )

    for side, begin in enumerate((0, row_count - halo)):
        rows = slice(begin, begin + halo)
        hout[side, :, :width] = fr_ref[rows, :].astype(jnp.float32)
        hout[side, :, width:] = own_lab_ref[rows, :].astype(jnp.float32)

    has = [t > 0, t < tms - 1]
    for side in range(2):
        @pl.when(has[side])
        def _(side=side):
            halo_copy(side).start()

    frame = lax.broadcasted_iota(jnp.int32, (wide, LANES), 0) + (t * row_count - halo)
    valid_ref[...] = jnp.where((frame >= 0) & (frame < len_ref[0]), 1.0, 0.0)
    x_ref[halo : halo + row_count, :] = fr_ref[...]
    lab_ref[rim : rim + row_count, :] = own_lab_ref[...].astype(jnp.float32)
    stat[...] = jnp.zeros_like(stat)
    f_ref[...] = jnp.full_like(f_ref, -jnp.inf)

    for side in range(2):
        @pl.when(has[side])
        def _(side=side):
            halo_copy(1 - side).wait_recv()

        @pl.when(jnp.logical_not(has[side]))
        def _(side=side):
            hin[side] = jnp.zeros((halo, hin.shape[2]), jnp.float32)

    x_ref[:halo, :] = hin[0, :, :width].astype(jnp.bfloat16)
    x_ref[halo + row_count :, :] = hin[1, :, :width].astype(jnp.bfloat16)
    lab_ref[:rim, :] = hin[0, halo - rim :, width:]
    lab_ref[rim + row_count :, :] = hin[1, :rim, width:]

    def score(c, carry):
        rows = pl.ds(pl.multiple_of(c * 2 * LANES, 2 * LANES), 2 * LANES)
        part = lax.dot_general(
            x_ref[...],
            qu_ref[rows, :],
            (((1,), (1,)), ((), ())),
            preferred_element_type=jnp.float32,
        )
        for h in range(2):
            one = part[:, h * LANES : (h + 1) * LANES] * scale
            sc_ref[2 * c + h] = jnp.where(valid_ref[...] > 0, one, 0.0)
        return carry

    lax.fori_loop(0, tiles // 2, score, 0)

    def smoothed(c, carry):
        taps = spread_taps(kern_ref, at(c))

        def body(g, carry):
            base = pl.multiple_of(g * block, block)
            sums = tap_block(lambda o: sc_ref[c, pl.ds(base + o, 8), :], taps, False)
            for i in range(GROUPS):
                rows = pl.ds(base + 8 * i, 8)
                e_ref[c, rows, :] = sums[i]
                f_ref[rows, :] = jnp.maximum(f_ref[rows, :], sums[i])
            return carry

        return lax.fori_loop(0, ext // block, body, carry)

    lax.fori_loop(0, tiles, smoothed, 0)

    diagonal = lax.broadcasted_iota(jnp.int32, (block, LANES), 0) == lax.broadcasted_iota(
        jnp.int32, (block, LANES), 1
    )

    def finish(g, carry):
        rows = pl.ds(pl.multiple_of(g * block, block), block)
        top = jnp.max(f_ref[rows, :], axis=1, keepdims=True)
        top = jnp.broadcast_to(top, (block, LANES))
        total = jnp.zeros((block, LANES), jnp.float32)
        for c in range(tiles):
            e = jnp.exp(e_ref[c, rows, :] - top)
            e_ref[c, rows, :] = e
            total = total + e
        total = jnp.broadcast_to(jnp.sum(total, axis=1, keepdims=True), (block, LANES))
        for i, value in enumerate((top, total)):
            picked = jnp.where(diagonal, value, 0.0)
            stat[0, i, pl.ds(g, 1), :] = jnp.sum(picked, axis=0, keepdims=True)
        return carry

    lax.fori_loop(0, ext // block, finish, 0)

    def stat_copy(k):
        bit = lax.rem(y // (1 << k), 2)
        device = {"query": y + (1 - 2 * bit) * (1 << k)}
        return copy(stat.at[k], stat_in.at[k], s_send.at[k], s_recv.at[k], device)

    rounds = peers.bit_length() - 1
    for k in range(rounds):
        stat_copy(k).start()
        stat_copy(k).wait_recv()
        top = jnp.maximum(stat[k, 0], stat_in[k, 0])
        stat[k + 1, 0] = top
        stat[k + 1, 1] = stat[k, 1] * jnp.exp(stat[k, 0] - top) + stat_in[k, 1] * jnp.exp(
            stat_in[k, 0] - top
        )
    stat[rounds, 1] = jnp.exp(stat[0, 0] - stat[rounds, 0]) / stat[rounds, 1]

    def widen(g, carry):
        rows = pl.ds(pl.multiple_of(g * block, block), block)
        row = jnp.broadcast_to(stat[rounds, 1, pl.ds(g, 1), :], (block, LANES))
        factor = jnp.sum(jnp.where(diagonal, row, 0.0), axis=1, keepdims=True)
        factor = jnp.broadcast_to(factor, (block, LANES))
        valid = valid_ref[pl.ds(pl.multiple_of(g * block, block) + rim, block), :] > 0
        f_ref[rows, :] = jnp.where(valid, factor, -1.0)
        return carry

    lax.fori_loop(0, ext // block, widen, 0)

    def map_gradient(c):
        first = (lane + c * chunk).astype(jnp.float32)

        def body(g, carry):
            for i in range(GROUPS):
                rows = pl.ds(pl.multiple_of(g * block + 8 * i, 8), 8)
                hit = jnp.where(lab_ref[rows, :] == first, 1.0, 0.0)
                factor = f_ref[rows, :]
                value = e_ref[c, rows, :] * jnp.maximum(factor, 0.0) - hit
                grad[rows, :] = jnp.where(factor >= 0.0, value, 0.0)
            return carry

        lax.fori_loop(0, ext // block, body, 0)

    def score_gradient(c):
        taps = spread_taps(kern_ref, at(c))

        def body(g, carry):
            base = pl.multiple_of(g * block, block)
            sums = tap_block(lambda o: grad[pl.ds(base + o, 8), :], taps, True)
            valid = f_ref[pl.ds(base + rim, block), :] >= 0.0
            total = jnp.where(valid, jnp.concatenate(sums, axis=0), 0.0)
            sg_ref[pl.ds(base, block), at(c)] = total.astype(jnp.bfloat16)
            return carry

        lax.fori_loop(0, row_count // block, body, 0)

    def tap_gradient(c):
        def body(g, sums):
            base = pl.multiple_of(g * block, block)
            held = [grad[pl.ds(base + rim + 8 * i, 8), :] for i in range(GROUPS)]
            sums = list(sums)
            for o in range(8 * (GROUPS - 1) + taps_n):
                v = sc_ref[c, pl.ds(base + rim + o, 8), :]
                for i in range(GROUPS):
                    j = o - 8 * i
                    if 0 <= j < taps_n:
                        sums[j] = sums[j] + held[i] * v
            return tuple(sums)

        zero = jnp.zeros((8, LANES), jnp.float32)
        sums = lax.fori_loop(0, row_count // block, body, (zero,) * taps_n)
        for j in range(taps_n):
            ksum[j : j + 1, :] = jnp.sum(sums[j], axis=0, keepdims=True)

    def start(c):
        map_gradient(c)
        score_gradient(c)
        tap_gradient(c)
        part = lax.dot_general(
            sg_ref[:, at(c)],
            fr_ref[...],
            (((0,), (0,)), ((), ())),
            preferred_element_type=jnp.float32,
        )
        for p in range(recs):
            j = bit_reversed(p, bits)
            acc[0][p, at(c), :] = part[:, j * cols : (j + 1) * cols]
        kacc[0][c] = ksum[...]
        for one in rec_copies(0, c):
            one.start()

    def exchange(k, c):
        total, ktotal = summed(k - 1, c)
        acc[k][:, at(c), :] = total
        kacc[k][c] = ktotal
        for one in rec_copies(k, c):
            one.start()

    def gather_in(c):
        total, ktotal = summed(bits - 1, c)
        mid[at(c), :] = total[0]
        kmid[c] = ktotal

        @pl.when(jnp.logical_not(is_end))
        def _():
            for one in inward_copies(c, False):
                one.wait_recv()
            mid[at(c), :] += outer[at(c), :]
            kmid[c] += kouter[c]

        @pl.when(is_mid)
        def _():
            for one in inward_copies(c, True):
                one.start()

        @pl.when(jnp.logical_not(is_mid))
        def _():
            for one in inward_copies(c, False):
                one.start()

    def spread_out(c):
        for one in inward_copies(c, True):
            one.wait_recv()

        @pl.when(is_mid)
        def _():
            inner[at(c), :] += mid[at(c), :]
            kinner[c] += kmid[c]

        @pl.when(jnp.logical_not(is_end))
        def _():
            for one in outward_copies(c):
                one.start()

        gq_ref[at(c), :] = (inner[at(c), :] * scale).astype(gq_ref.dtype)
        gk_ref[:, at(c)] = kinner[c]

    def send_frames():
        for d in range(1, peers):
            f_compute(lax.rem(y + d, peers))
            f_copy(d).start()

    reach = half - 1
    away = jnp.where(low, reach - t, t - half)
    in_lag = bits + 1 + 2 * (reach - away)
    out_lag = bits + 3 + 2 * (reach + away)
    last_lag = bits + 3 + 4 * reach
    stages = [(0, start), (out_lag, spread_out), (in_lag, gather_in)]
    stages += [(k, functools.partial(exchange, k)) for k in range(bits - 1, 0, -1)]

    def step(s, carry):
        for delay, stage in stages:
            @pl.when((s >= delay) & (s < count + delay))
            def _(stage=stage, delay=delay):
                stage(s - delay)

        @pl.when(s == count - 1)
        def _():
            send_frames()

        @pl.when(s == count + 1)
        def _():
            f_compute(y)

        return carry

    lax.fori_loop(0, count + last_lag, step, 0)

    for d in range(1, peers):
        f_copy(d).wait_recv()
    total = fpart[y]
    for d in range(1, peers):
        total = total + fin[d - 1]
    gf_ref[...] = (total * scale).astype(gf_ref.dtype)
    for d in range(1, peers):
        f_copy(d).wait_send()

    def drain(c, carry):
        for k in range(bits):
            for one in rec_copies(k, c):
                one.wait_send()
        for one in inward_copies(c, False):
            one.wait_send()

        @pl.when(jnp.logical_not(is_end))
        def _():
            for one in outward_copies(c):
                one.wait_send()

        return carry

    lax.fori_loop(0, count, drain, 0)
    for k in range(rounds):
        stat_copy(k).wait_send()
    for side in range(2):
        @pl.when(has[side])
        def _(side=side):
            halo_copy(side).wait_send()


def gradients(labels, lengths, frame_rows, queries, kernel, scale):
    tms, peers, recs = (lax.axis_size("tm"), lax.axis_size("query"), lax.axis_size("rec"))
    bits = recs.bit_length() - 1
    row_count, width = frame_rows.shape
    query_count = queries.shape[0]
    taps = kernel.shape[0]
    chunk = LANES
    count = query_count // chunk
    cols, fcols = (width // recs, width // peers)
    rim = taps // 2
    ext, wide = (row_count + 2 * rim, row_count + 4 * rim)
    rounds = peers.bit_length() - 1
    stat_rows = (ext // (8 * GROUPS) + 7) // 8 * 8
    f32 = jnp.float32
    small = pltpu.VMEM((count, taps, chunk), f32)
    block = pltpu.VMEM((query_count, cols), f32)
    scratch = [pltpu.VMEM((recs >> k, query_count, cols), f32) for k in range(bits)]
    scratch += [pltpu.VMEM((recs >> (k + 1), query_count, cols), f32) for k in range(bits)]
    scratch += [small] * (2 * bits) + [block] * 3 + [small] * 3
    scratch += [
        pltpu.VMEM((peers, row_count, fcols), f32),
        pltpu.VMEM((peers - 1, row_count, fcols), f32),
        pltpu.VMEM((row_count, query_count), jnp.bfloat16),
        pltpu.VMEM((ext, chunk), f32),
        pltpu.VMEM((taps, chunk), f32),
        pltpu.VMEM((count, wide, chunk), f32),
        pltpu.VMEM((count, ext, chunk), f32),
        pltpu.VMEM((ext, chunk), f32),
        pltpu.VMEM((ext, chunk), f32),
        pltpu.VMEM((wide, chunk), f32),
        pltpu.VMEM((wide, width), jnp.bfloat16),
        pltpu.VMEM((2, 2 * rim, width + LANES), f32),
        pltpu.VMEM((2, 2 * rim, width + LANES), f32),
        pltpu.VMEM((rounds + 1, 2, stat_rows, LANES), f32),
        pltpu.VMEM((rounds, 2, stat_rows, LANES), f32),
    ]
    dma = pltpu.SemaphoreType.DMA
    scratch += [dma((bits, 2, count))] * 2 + [dma((2, count))] * 4 + [dma((peers - 1,))] * 2
    scratch += [dma((2,))] * 2 + [dma((rounds,))] * 2
    vmem = pl.BlockSpec(memory_space=pltpu.VMEM)
    return pl.pallas_call(
        functools.partial(gradient_kernel, (tms, peers, recs, chunk), scale),
        out_shape=(
            jax.ShapeDtypeStruct((row_count, fcols), jnp.bfloat16),
            jax.ShapeDtypeStruct((query_count, cols), jnp.bfloat16),
            jax.ShapeDtypeStruct((taps, query_count), f32),
        ),
        in_specs=[vmem, pl.BlockSpec(memory_space=pltpu.SMEM), vmem, vmem, vmem],
        out_specs=(vmem,) * 3,
        scratch_shapes=scratch,
        compiler_params=pltpu.CompilerParams(
            collective_id=0, has_side_effects=True, vmem_limit_bytes=60 * 1024 * 1024
        ),
        name="gradients",
    )(labels, lengths, frame_rows, queries, kernel)


def per_device(frames, queries, kernel, labels, lengths):
    frame_rows = frames[0]
    row_count, width = frame_rows.shape
    logit_scale = 10.0 / math.sqrt(width)
    label_wide = jnp.broadcast_to(labels[0][:, None], (row_count, LANES))
    grad_frames, grad_queries, grad_kernel = gradients(
        label_wide, lengths, frame_rows, queries, kernel, logit_scale
    )
    return (grad_frames[None], grad_queries, grad_kernel)


def solution(mesh):
    in_specs = (P("rec", "tm", None), P("query", None), P(None, "query"), P("rec", "tm"), P("rec"))
    out_specs = (P("rec", "tm", "query"), P("query", "rec"), P(None, "query"))
    return jax.shard_map(
        per_device, mesh=mesh, in_specs=in_specs, out_specs=out_specs, check_vma=False
    )
```
